32 devices in a mesh: groups: 2 (over y), ctx: 4 (over z), dp: 2 (over x), rep: 2 (over core).
Axes of the slice: x: 2, y: 2, z: 4, core: 2. Of those that a mesh axis runs over, the one named last changes fastest.
Arguments:
- features: float32 [8, 4096, 128], P(('groups', 'dp', 'rep'), 'ctx'), parts along dimension 0, may hold values from -6 to 6
- cotangent: float32 [8, 4096, 128], P(('groups', 'dp', 'rep'), 'ctx'), parts along dimension 0, may hold values from -6 to 6
- norm_gains: float32 [2, 128], replicated, may hold values from 0.5 to 1.5
- depth_taps: float32 [2, 7, 128], replicated, may hold values from -2 to 2
- w_in: float32 [2, 128, 256], replicated, may hold values from -0.5 to 0.5
- w_out: float32 [2, 256, 128], replicated, may hold values from -0.375 to 0.375
Outputs:
- grad_features: float32 [8, 4096, 128], P(('groups', 'dp', 'rep'), 'ctx'), parts along dimension 0
- grad_gains: float32 [4, 128], P('groups'), parts along dimension 0
- grad_taps: float32 [4, 7, 128], P('groups'), parts along dimension 0
- grad_w_in: float32 [4, 128, 256], P('groups'), parts along dimension 0
- grad_w_out: float32 [4, 256, 128], P('groups'), parts along dimension 0
The draws below stay inside these ranges and needn't reach their ends.
There are 2 independent parts, one for each index of `groups`. The reference program is written for one: setup_inputs(seed, part) draws one part's arguments, and reference() takes and returns one part's arrays. A program takes and returns all parts, laid end to end along the dimension named above; an argument that names none is the same for every part. Nothing has to cross between parts.
All inputs are finite; a program needn't handle non-finite values.
Results may differ from the reference program's by a relative error of at most 0.0001.
Values sent between devices are 32-bit elements; how exact they have to be, the bound alone decides.
A program may use at most 64 MiB of HBM per device.

```python
import jax
import jax.numpy as jnp
from jax import lax

C = 128
HID = 256
KSIZE = 7
FIRST_SPACING = 16
SECOND_SPACING = 256
BLOCKS = 2
LENGTH = 4096
EVENTS = 4


def shard_levels(rng, dims, shards, least, largest):
    factor_of = 1.0
    for dim, blocks in shards:
        heights = jax.random.uniform(jax.random.fold_in(jax.random.fold_in(rng, 6), dim), (blocks,), jnp.float32, least / len(shards), largest / len(shards))
        factor_of = factor_of * jnp.repeat(jnp.exp(heights), dims[dim] // blocks).reshape((-1,) + (1,) * (len(dims) - 1 - dim))
    return factor_of


def noise(rng, shape, deviation, reach, pieces=(), kind=jnp.bfloat16):
    drawn = jax.random.normal(rng, shape, jnp.float32) * deviation
    if len(pieces) > 0:
        drawn = shard_levels(rng, shape, pieces, -0.22, 0.18) * drawn
    return jnp.clip(drawn, min=-reach, max=reach).astype(kind)


def setup_inputs(seed: int = 0, part: int = 0) -> dict:
    splits = jax.random.split(jax.random.key(seed), 7)
    part_splits = jax.random.split(jax.random.fold_in(splits[6], part), 7)
    features = noise(part_splits[0], (EVENTS, LENGTH, C), 1.0, 6.0, ((0, 4), (1, 4)), jnp.float32)
    cotangent = noise(part_splits[1], (EVENTS, LENGTH, C), 1.0, 6.0, ((0, 4), (1, 4)), jnp.float32)
    norm_gains = jnp.clip(1.0 + 0.1 * jax.random.normal(splits[2], (BLOCKS, C), jnp.float32), 0.5, 1.5)
    depth_taps = noise(splits[3], (BLOCKS, KSIZE, C), KSIZE ** -0.5, 2.0, (), jnp.float32)
    w_in = noise(splits[4], (BLOCKS, C, HID), C ** -0.5, 0.5, (), jnp.float32)
    w_out = noise(splits[5], (BLOCKS, HID, C), HID ** -0.5, 0.375, (), jnp.float32)
    return dict(features=features, cotangent=cotangent, norm_gains=norm_gains, depth_taps=depth_taps, w_in=w_in, w_out=w_out)


STABILIZER = 1e-06

def rms_norm(stream, gain_vec):
    scale = lax.rsqrt(lax.optimization_barrier(jnp.mean(stream * stream, axis=-1, keepdims=True)) + STABILIZER)
    return stream * scale * gain_vec

def depth_sweep(padded, tap_weights, dilation, row_count):
    total = tap_weights[0] * padded[:, 0:row_count]
    for offset in range(1, tap_weights.shape[0]):
        total = total + tap_weights[offset] * padded[:, offset * dilation:offset * dilation + row_count]
    return total

def tower(features, norm_gains, depth_taps, w_in, w_out):
    spacing_list = (FIRST_SPACING, SECOND_SPACING)
    stream = features
    for block_index in range(BLOCKS):
        dilation = spacing_list[block_index]
        rim_width = KSIZE // 2 * dilation
        normed = rms_norm(stream, norm_gains[block_index])
        padded = jnp.pad(normed, ((0, 0), (rim_width, rim_width), (0, 0)))
        conv_out = depth_sweep(padded, depth_taps[block_index], dilation, stream.shape[1])
        pre_act = jnp.einsum('elc,ch->elh', conv_out, w_in[block_index], precision=lax.Precision.HIGHEST)
        act_out = jax.nn.silu(pre_act)
        stream = stream + jnp.einsum('elh,hc->elc', act_out, w_out[block_index], precision=lax.Precision.HIGHEST)
    return stream

def reference(features, cotangent, norm_gains, depth_taps, w_in, w_out):
    result, pullback = jax.vjp(tower, features, norm_gains, depth_taps, w_in, w_out)
    grad_x, grad_g, grad_t, input_gradient, grad_o = pullback(cotangent)
    return (grad_x, grad_g, grad_t, input_gradient, grad_o)
```

```python
import functools

import jax
import jax.numpy as jnp
from jax import lax
from jax.experimental import pallas as pl
from jax.experimental.pallas import tpu as pltpu
from jax.sharding import PartitionSpec as P

D1 = 16
D2 = 256
TAPS = 7
HALF = TAPS // 2
CHUNKS = 4
RES = D2 // CHUNKS
EPS = 1e-06
F32 = jnp.float32
BF16 = jnp.bfloat16
MESH = pl.DeviceIdType.MESH
ORDER = (1, 2, 0, 3)

NN = (((1,), (0,)), ((), ()))
NT = (((1,), (1,)), ((), ()))
TN = (((0,), (0,)), ((), ()))


def split(v):
    high = v.astype(BF16)
    return high, (v - high.astype(F32)).astype(BF16)


def dot3(ah, al, bh, bl, dims):
    def dot(a, b):
        return lax.dot_general(a, b, dims, preferred_element_type=F32)

    return dot(ah, bh) + (dot(ah, bl) + dot(al, bh))


def inv_rms(v):
    return lax.rsqrt(jnp.mean(v * v, axis=-1, keepdims=True) + EPS)


def silu_pair(pre):
    s = 1.0 / (1.0 + jnp.exp(-pre))
    act = pre * s
    return act, s + act * (1.0 - s)


def kernel(
    nctx, ndp, nrep, rows_total, grad_rows,
    x_ref, ct_ref, gain_ref, taps_ref, win_ref, wout_ref,
    gx_ref, gg_ref, gt_ref, gwi_ref, gwo_ref,
    pad1, gpad1, pad2, gpad2, st1, g1,
    wih, wil, woh, wol,
    ch, cl, ah, al, dact, gh, gl, ph, plo,
    gbuf, obuf, rec_a, rec_b, rec_c, small, sm_a, sm_b, sm_c,
    send_sem, recv_sem,
):
    segs = rows_total // D2
    crow = segs * RES
    rim = HALF * D1
    zi = lax.axis_index("ctx")
    di = lax.axis_index("dp")
    ri = lax.axis_index("rep")
    has_left = zi > 0
    has_right = zi < nctx - 1
    left = lax.rem(zi + nctx - 1, nctx)
    right = lax.rem(zi + 1, nctx)
    count = [0]
    pending = []

    def remote(src, dst, device):
        i = count[0]
        count[0] += 1
        return pltpu.make_async_remote_copy(
            src_ref=src, dst_ref=dst, send_sem=send_sem.at[i], recv_sem=recv_sem.at[i],
            device_id=device, device_id_type=MESH,
        )

    barrier = pltpu.get_barrier_semaphore()
    greeted = 0
    for axis, me, n in (("ctx", zi, nctx), ("dp", di, ndp), ("rep", ri, nrep)):
        for o in range(1, n):
            pl.semaphore_signal(
                barrier, inc=1, device_id={axis: lax.rem(me + o, n)}, device_id_type=MESH
            )
            greeted += 1

    gain1 = gain_ref[0:1, :]
    gain2 = gain_ref[1:2, :]

    def norm_rows(lo, n):
        v = x_ref[0, lo:lo + n, :]
        pad1[rim + lo:rim + lo + n, :] = v * inv_rms(v) * gain1

    norm_rows(0, rim)
    norm_rows(rows_total - rim, rim)
    pl.semaphore_wait(barrier, greeted)

    class Halo:
        def __init__(self, to_right_src, to_right_dst, to_left_src, to_left_dst):
            self.r = remote(to_right_src, to_right_dst, {"ctx": right})
            self.l = remote(to_left_src, to_left_dst, {"ctx": left})

        def start(self):
            @pl.when(has_right)
            def _():
                self.r.start()

            @pl.when(has_left)
            def _():
                self.l.start()

            pending.append(self)

        def wait(self):
            @pl.when(has_left)
            def _():
                self.r.wait_recv()

            @pl.when(has_right)
            def _():
                self.l.wait_recv()

        def finish(self):
            @pl.when(has_right)
            def _():
                self.r.wait_send()

            @pl.when(has_left)
            def _():
                self.l.wait_send()

    def rim_halo(ref):
        return Halo(
            ref.at[pl.ds(rows_total, rim)], ref.at[pl.ds(0, rim)],
            ref.at[pl.ds(rim, rim)], ref.at[pl.ds(rim + rows_total, rim)],
        )

    def seg_halo(ref, c):
        return Halo(
            ref.at[c, pl.ds(segs, HALF)], ref.at[c, pl.ds(0, HALF)],
            ref.at[c, pl.ds(HALF, HALF)], ref.at[c, pl.ds(HALF + segs, HALF)],
        )

    halo1 = rim_halo(pad1)
    halo1.start()

    @pl.when(zi == 0)
    def _():
        pad1[0:rim, :] = jnp.zeros((rim, 128), F32)
        gpad1[0:rim, :] = jnp.zeros((rim, 128), F32)
        pad2[:, 0:HALF] = jnp.zeros((CHUNKS, HALF, RES, 128), F32)
        gpad2[:, 0:HALF] = jnp.zeros((CHUNKS, HALF, RES, 128), F32)

    @pl.when(zi == nctx - 1)
    def _():
        pad1[rim + rows_total:, :] = jnp.zeros((rim, 128), F32)
        gpad1[rim + rows_total:, :] = jnp.zeros((rim, 128), F32)
        pad2[:, HALF + segs:] = jnp.zeros((CHUNKS, HALF, RES, 128), F32)
        gpad2[:, HALF + segs:] = jnp.zeros((CHUNKS, HALF, RES, 128), F32)

    norm_rows(rim, rows_total - 2 * rim)
    for b in range(2):
        wih[b], wil[b] = split(win_ref[b])
        woh[b], wol[b] = split(wout_ref[b])

    def gather(ref, c, base):
        return jnp.concatenate(
            [ref[base + j * D2 + c * RES:base + j * D2 + (c + 1) * RES, :] for j in range(segs)],
            axis=0,
        )

    def tap(b, k):
        return taps_ref[b, k:k + 1, :]

    def forward_tail(b, c, conv):
        at = pl.ds(c * crow, crow)
        cth, ctl = split(conv)
        ch[b, at], cl[b, at] = cth, ctl
        pre = dot3(cth, ctl, wih[b], wil[b], NN)
        act, slope = silu_pair(pre)
        dact[b, at] = slope
        ath, atl = split(act)
        ah[b, at], al[b, at] = ath, atl

    def backward_head(b, c, g):
        at = pl.ds(c * crow, crow)
        gth, gtl = split(g)
        gh[b, at], gl[b, at] = gth, gtl
        gpre = dot3(gth, gtl, woh[b], wol[b], NT) * dact[b, at]
        pth, ptl = split(gpre)
        ph[b, at], plo[b, at] = pth, ptl
        return dot3(pth, ptl, wih[b], wil[b], NT)

    def weight_grads(b):
        gwi = dot3(ch[b], cl[b], ph[b], plo[b], TN)
        gbuf[b, 0:128, :] = gwi[:, 0:128]
        gbuf[b, 128:256, :] = gwi[:, 128:256]
        gbuf[b, 256:512, :] = dot3(ah[b], al[b], gh[b], gl[b], TN)

    halo2 = [seg_halo(pad2, c) for c in range(CHUNKS)]
    waited = False
    for c in ORDER:
        if c in (0, CHUNKS - 1) and not waited:
            halo1.wait()
            waited = True
        conv = tap(0, 0) * gather(pad1, c, 0)
        for k in range(1, TAPS):
            conv = conv + tap(0, k) * gather(pad1, c, k * D1)
        forward_tail(0, c, conv)
        at = pl.ds(c * crow, crow)
        s = gather(x_ref.at[0], c, 0) + dot3(ah[0, at], al[0, at], woh[0], wol[0], NN)
        st1[at] = s
        pad2[c, HALF:HALF + segs] = (s * inv_rms(s) * gain2).reshape(segs, RES, 128)
        halo2[c].start()

    ghalo2 = [seg_halo(gpad2, c) for c in range(CHUNKS)]
    for c in ORDER:
        halo2[c].wait()
        conv = tap(1, 0) * pad2[c, 0:segs].reshape(crow, 128)
        for k in range(1, TAPS):
            conv = conv + tap(1, k) * pad2[c, k:k + segs].reshape(crow, 128)
        forward_tail(1, c, conv)
        gconv = backward_head(1, c, gather(ct_ref.at[0], c, 0))
        gpad2[c, HALF:HALF + segs] = gconv.reshape(segs, RES, 128)
        ghalo2[c].start()

    half = grad_rows // nrep
    quarter = half // ndp
    piece = quarter // nctx
    axes = (
        ("rep", ri, nrep, rec_a, sm_a, half, 0),
        ("dp", di, ndp, rec_b, sm_b, quarter, ri * half),
        ("ctx", zi, nctx, rec_c, sm_c, piece, ri * half + di * quarter),
    )

    def rows_at(start, size):
        return pl.ds(pl.multiple_of(start, 8), size)

    def scatter_start(b, level):
        axis, me, n, rec, _, size, base = axes[level]
        copies = []
        for o in range(1, n):
            peer = lax.rem(me + o, n)
            copy = remote(
                gbuf.at[b, rows_at(base + peer * size, size)], rec.at[b, o - 1], {axis: peer}
            )
            copy.start()
            copies.append(copy)
        pending.append(copies)
        return copies

    def scatter_end(b, level, copies):
        axis, me, n, rec, _, size, base = axes[level]
        own = rows_at(base + me * size, size)
        total = gbuf[b, own, :]
        for o in range(1, n):
            copies[o - 1].wait_recv()
            total = total + rec[b, o - 1]
        if level == 2:
            obuf[b, own, :] = total
        else:
            gbuf[b, own, :] = total

    def gather_start(b, level):
        axis, me, n, _, _, size, base = axes[level]
        own = rows_at(base + me * size, size)
        copies = []
        for o in range(1, n):
            peer = lax.rem(me + o, n)
            copy = remote(obuf.at[b, own], obuf.at[b, own], {axis: peer})
            copy.start()
            copies.append(copy)
        pending.append(copies)
        return copies

    def arrive(copies):
        for copy in copies:
            copy.wait_recv()

    def small_start(level):
        axis, me, n, _, slots, _, _ = axes[level]
        slots[me] = small[...]
        copies = []
        for o in range(1, n):
            peer = lax.rem(me + o, n)
            copy = remote(slots.at[me], slots.at[me], {axis: peer})
            copy.start()
            copies.append(copy)
        pending.append(copies)
        return copies

    def small_end(level, copies):
        n, slots = axes[level][2], axes[level][4]
        arrive(copies)
        total = slots[0]
        for i in range(1, n):
            total = total + slots[i]
        small[...] = total

    weight_grads(1)
    red2 = scatter_start(1, 0)
    for k in range(TAPS):
        total = jnp.zeros((1, 128), F32)
        for c in range(CHUNKS):
            both = gpad2[c, HALF:HALF + segs] * pad2[c, k:k + segs]
            total = total + jnp.sum(both.reshape(crow, 128), axis=0, keepdims=True)
        small[k:k + 1, :] = total

    gain_sum = jnp.zeros((1, 128), F32)
    for step, c in enumerate(ORDER):
        ghalo2[c].wait()
        at = pl.ds(c * crow, crow)
        gnorm = tap(1, TAPS - 1) * gpad2[c, 0:segs].reshape(crow, 128)
        for k in range(1, TAPS):
            gnorm = gnorm + tap(1, TAPS - 1 - k) * gpad2[c, k:k + segs].reshape(crow, 128)
        s = st1[at]
        r = inv_rms(s)
        xhat = s * r
        gain_sum = gain_sum + jnp.sum(gnorm * xhat, axis=0, keepdims=True)
        q = gnorm * gain2
        g = gather(ct_ref.at[0], c, 0) + r * (q - xhat * jnp.mean(q * xhat, axis=-1, keepdims=True))
        gconv = backward_head(0, c, g)
        for j in range(segs):
            lo = j * D2 + c * RES
            g1[lo:lo + RES, :] = g[j * RES:(j + 1) * RES, :]
            gpad1[rim + lo:rim + lo + RES, :] = gconv[j * RES:(j + 1) * RES, :]
        if step == 1:
            scatter_end(1, 0, red2)
            red2 = scatter_start(1, 1)
    small[7:8, :] = gain_sum
    ghalo1 = rim_halo(gpad1)
    ghalo1.start()
    weight_grads(0)
    red1 = scatter_start(0, 0)
    scatter_end(1, 1, red2)
    red2 = scatter_start(1, 2)
    for k in range(TAPS):
        both = gpad1[rim:rim + rows_total, :] * pad1[k * D1:k * D1 + rows_total, :]
        small[8 + k:9 + k, :] = jnp.sum(both, axis=0, keepdims=True)

    scatter_end(0, 0, red1)
    red1 = scatter_start(0, 1)

    gain_sum = jnp.zeros((1, 128), F32)
    waited = False
    blocks = rows_total // D2
    for q_i in [i for i in range(1, blocks - 1)] + [0, blocks - 1]:
        if q_i in (0, blocks - 1) and not waited:
            ghalo1.wait()
            waited = True
        lo = q_i * D2
        gnorm = tap(0, TAPS - 1) * gpad1[lo:lo + D2, :]
        for k in range(1, TAPS):
            gnorm = gnorm + tap(0, TAPS - 1 - k) * gpad1[lo + k * D1:lo + k * D1 + D2, :]
        s = x_ref[0, lo:lo + D2, :]
        r = inv_rms(s)
        xhat = s * r
        gain_sum = gain_sum + jnp.sum(gnorm * xhat, axis=0, keepdims=True)
        q = gnorm * gain1
        gx_ref[0, lo:lo + D2, :] = g1[lo:lo + D2, :] + r * (
            q - xhat * jnp.mean(q * xhat, axis=-1, keepdims=True)
        )
    small[15:16, :] = gain_sum

    tiny = small_start(0)
    scatter_end(1, 2, red2)
    all2 = gather_start(1, 2)
    scatter_end(0, 1, red1)
    red1 = scatter_start(0, 2)
    small_end(0, tiny)
    tiny = small_start(1)
    arrive(all2)
    all2 = gather_start(1, 1)
    scatter_end(0, 2, red1)
    all1 = gather_start(0, 2)
    small_end(1, tiny)
    tiny = small_start(2)
    arrive(all2)
    all2 = gather_start(1, 0)
    arrive(all1)
    all1 = gather_start(0, 1)
    small_end(2, tiny)
    arrive(all2)

    def write_out(b):
        gwi_ref[b, :, 0:128] = obuf[b, 0:128, :]
        gwi_ref[b, :, 128:256] = obuf[b, 128:256, :]
        gwo_ref[b] = obuf[b, 256:512, :]

    write_out(1)
    gt_ref[1] = small[0:7, :]
    gg_ref[1:2, :] = small[7:8, :]
    gt_ref[0] = small[8:15, :]
    gg_ref[0:1, :] = small[15:16, :]
    arrive(all1)
    all1 = gather_start(0, 0)
    arrive(all1)
    write_out(0)

    for item in pending:
        if isinstance(item, list):
            for copy in item:
                copy.wait_send()
        else:
            item.finish()


def local(nctx, ndp, nrep, features, cotangent, norm_gains, depth_taps, w_in, w_out):
    rows = features.shape[1]
    unit = 8 * nctx * ndp * nrep
    grad_rows = -(-512 // unit) * unit
    half = grad_rows // nrep
    quarter = half // ndp
    piece = quarter // nctx
    rim = HALF * D1
    wide = rows // D2 + 2 * HALF
    sems = 4 + 4 * CHUNKS + 5 * (nctx + ndp + nrep)
    vmem = pltpu.VMEM

    def peers(n):
        return max(n - 1, 1)

    return pl.pallas_call(
        functools.partial(kernel, nctx, ndp, nrep, rows, grad_rows),
        out_shape=(
            jax.ShapeDtypeStruct(features.shape, F32),
            jax.ShapeDtypeStruct(norm_gains.shape, F32),
            jax.ShapeDtypeStruct(depth_taps.shape, F32),
            jax.ShapeDtypeStruct(w_in.shape, F32),
            jax.ShapeDtypeStruct(w_out.shape, F32),
        ),
        in_specs=[pl.BlockSpec(memory_space=vmem)] * 6,
        out_specs=tuple([pl.BlockSpec(memory_space=vmem)] * 5),
        scratch_shapes=[
            vmem((rows + 2 * rim, 128), F32),
            vmem((rows + 2 * rim, 128), F32),
            vmem((CHUNKS, wide, RES, 128), F32),
            vmem((CHUNKS, wide, RES, 128), F32),
            vmem((rows, 128), F32),
            vmem((rows, 128), F32),
            vmem((2, 128, 256), BF16),
            vmem((2, 128, 256), BF16),
            vmem((2, 256, 128), BF16),
            vmem((2, 256, 128), BF16),
            vmem((2, rows, 128), BF16),
            vmem((2, rows, 128), BF16),
            vmem((2, rows, 256), BF16),
            vmem((2, rows, 256), BF16),
            vmem((2, rows, 256), F32),
            vmem((2, rows, 128), BF16),
            vmem((2, rows, 128), BF16),
            vmem((2, rows, 256), BF16),
            vmem((2, rows, 256), BF16),
            vmem((2, grad_rows, 128), F32),
            vmem((2, grad_rows, 128), F32),
            vmem((2, peers(nrep), half, 128), F32),
            vmem((2, peers(ndp), quarter, 128), F32),
            vmem((2, peers(nctx), piece, 128), F32),
            vmem((16, 128), F32),
            vmem((nrep, 16, 128), F32),
            vmem((ndp, 16, 128), F32),
            vmem((nctx, 16, 128), F32),
            pltpu.SemaphoreType.DMA((sems,)),
            pltpu.SemaphoreType.DMA((sems,)),
        ],
        compiler_params=pltpu.CompilerParams(
            collective_id=0, has_side_effects=True, vmem_limit_bytes=40 * 1024 * 1024
        ),
    )(features, cotangent, norm_gains, depth_taps, w_in, w_out)


def solution(mesh):
    sizes = dict(mesh.shape)
    return jax.shard_map(
        functools.partial(local, sizes["ctx"], sizes["dp"], sizes["rep"]),
        mesh=mesh,
        in_specs=(
            P(("groups", "dp", "rep"), "ctx", None),
            P(("groups", "dp", "rep"), "ctx", None),
            P(),
            P(),
            P(),
            P(),
        ),
        out_specs=(
            P(("groups", "dp", "rep"), "ctx", None),
            P("groups", None),
            P("groups", None, None),
            P("groups", None, None),
            P("groups", None, None),
        ),
        check_vma=False,
    )
```

```python
import functools

import jax
import jax.numpy as jnp
from jax import lax
from jax.experimental import pallas as pl
from jax.experimental.pallas import tpu as pltpu
from jax.sharding import PartitionSpec as P

D1 = 16
D2 = 256
TAPS = 7
HALF = TAPS // 2
CHUNKS = 4
RES = D2 // CHUNKS
EPS = 1e-06
F32 = jnp.float32
BF16 = jnp.bfloat16
MESH = pl.DeviceIdType.MESH
ORDER = (1, 2, 0, 3)

NN = (((1,), (0,)), ((), ()))
TN = (((0,), (0,)), ((), ()))


def split(v):
    high = v.astype(BF16)
    return high, (v - high.astype(F32)).astype(BF16)


def dot(a, b, dims=NN):
    return lax.dot_general(a, b, dims, preferred_element_type=F32)


def expand(pair, dup, low):
    return dot(pair, dup) + dot(pair[:, 0:128], low)


def contract(high, low, cat):
    both = dot(high, cat)
    return both[:, 0:128] + (both[:, 128:256] + dot(low, cat[:, 0:128]))


def inv_rms(v):
    return lax.rsqrt(jnp.mean(v * v, axis=-1, keepdims=True) + EPS)


def silu_pair(pre):
    s = 1.0 / (1.0 + jnp.exp(-pre))
    act = pre * s
    return act, s + act * (1.0 - s)


def kernel(
    nctx, ndp, nrep, rows_total, grad_rows,
    x_hbm, ct_hbm, gain_hbm, taps_hbm, win_hbm, wout_hbm,
    gx_ref, gg_ref, gt_ref, gwi_ref, gwo_ref,
    x_ref, ct_ref, gain_ref, taps_ref, win_ref, wout_ref, load_sem,
    pad1, gpad1, pad2, gpad2, st1, g1,
    in_dup, in_low, out_cat, outt_dup, outt_low, int_cat,
    chl, ah, al, dact, ghl, ph, plo,
    gbuf, obuf, rec_a, rec_b, rec_c, small, sm_a, sm_b, sm_c,
    send_sem, recv_sem,
):
    segs = rows_total // D2
    crow = segs * RES
    rim = HALF * D1
    zi = lax.axis_index("ctx")
    di = lax.axis_index("dp")
    ri = lax.axis_index("rep")
    has_left = zi > 0
    has_right = zi < nctx - 1
    left = lax.rem(zi + nctx - 1, nctx)
    right = lax.rem(zi + 1, nctx)
    count = [0]
    pending = []

    def remote(src, dst, device):
        i = count[0]
        count[0] += 1
        return pltpu.make_async_remote_copy(
            src_ref=src, dst_ref=dst, send_sem=send_sem.at[i], recv_sem=recv_sem.at[i],
            device_id=device, device_id_type=MESH,
        )

    loads = [
        pltpu.make_async_copy(src, dst, load_sem.at[i])
        for i, (src, dst) in enumerate(
            (
                (gain_hbm, gain_ref), (x_hbm, x_ref), (taps_hbm, taps_ref),
                (win_hbm, win_ref), (wout_hbm, wout_ref), (ct_hbm, ct_ref),
            )
        )
    ]
    for load in loads:
        load.start()

    barrier = pltpu.get_barrier_semaphore()
    def on_rep(p):
        return {"rep": p}

    def on_dp(p):
        return {"dp": p}

    def on_ctx(p):
        return {"ctx": p}

    greeted = 0
    for place, me, n in ((on_ctx, zi, nctx), (on_dp, di, ndp), (on_rep, ri, nrep)):
        for o in range(1, n):
            pl.semaphore_signal(
                barrier, inc=1, device_id=place(lax.rem(me + o, n)), device_id_type=MESH
            )
            greeted += 1

    loads[0].wait()
    loads[1].wait()
    gain1 = gain_ref[0:1, :]
    gain2 = gain_ref[1:2, :]

    def norm_rows(lo, n):
        v = x_ref[0, lo:lo + n, :]
        pad1[rim + lo:rim + lo + n, :] = v * inv_rms(v) * gain1

    norm_rows(0, rim)
    norm_rows(rows_total - rim, rim)
    for load in loads[2:5]:
        load.wait()
    for b in range(2):
        high, low = split(win_ref[b])
        in_dup[b] = jnp.concatenate([high, high], axis=0)
        in_low[b] = low
        high, low = split(win_ref[b].T)
        int_cat[b] = jnp.concatenate([high, low], axis=1)
        high, low = split(wout_ref[b])
        out_cat[b] = jnp.concatenate([high, low], axis=1)
        high, low = split(wout_ref[b].T)
        outt_dup[b] = jnp.concatenate([high, high], axis=0)
        outt_low[b] = low
    pl.semaphore_wait(barrier, greeted)

    class Halo:
        def __init__(self, to_right_src, to_right_dst, to_left_src, to_left_dst):
            self.r = remote(to_right_src, to_right_dst, {"ctx": right})
            self.l = remote(to_left_src, to_left_dst, {"ctx": left})

        def start(self):
            @pl.when(has_right)
            def _():
                self.r.start()

            @pl.when(has_left)
            def _():
                self.l.start()

            pending.append(self)

        def wait(self):
            @pl.when(has_left)
            def _():
                self.r.wait_recv()

            @pl.when(has_right)
            def _():
                self.l.wait_recv()

        def finish(self):
            @pl.when(has_right)
            def _():
                self.r.wait_send()

            @pl.when(has_left)
            def _():
                self.l.wait_send()

    def rim_halo(ref):
        return Halo(
            ref.at[pl.ds(rows_total, rim)], ref.at[pl.ds(0, rim)],
            ref.at[pl.ds(rim, rim)], ref.at[pl.ds(rim + rows_total, rim)],
        )

    def seg_halo(ref, c):
        return Halo(
            ref.at[c, pl.ds(segs, HALF)], ref.at[c, pl.ds(0, HALF)],
            ref.at[c, pl.ds(HALF, HALF)], ref.at[c, pl.ds(HALF + segs, HALF)],
        )

    halo1 = rim_halo(pad1)
    halo1.start()

    @pl.when(zi == 0)
    def _():
        pad1[0:rim, :] = jnp.zeros((rim, 128), F32)
        gpad1[0:rim, :] = jnp.zeros((rim, 128), F32)
        pad2[:, 0:HALF] = jnp.zeros((CHUNKS, HALF, RES, 128), F32)
        gpad2[:, 0:HALF] = jnp.zeros((CHUNKS, HALF, RES, 128), F32)

    @pl.when(zi == nctx - 1)
    def _():
        pad1[rim + rows_total:, :] = jnp.zeros((rim, 128), F32)
        gpad1[rim + rows_total:, :] = jnp.zeros((rim, 128), F32)
        pad2[:, HALF + segs:] = jnp.zeros((CHUNKS, HALF, RES, 128), F32)
        gpad2[:, HALF + segs:] = jnp.zeros((CHUNKS, HALF, RES, 128), F32)

    norm_rows(rim, rows_total - 2 * rim)
    def gather(ref, c, base):
        return jnp.concatenate(
            [ref[base + j * D2 + c * RES:base + j * D2 + (c + 1) * RES, :] for j in range(segs)],
            axis=0,
        )

    def tap(b, k):
        return taps_ref[k, b:b + 1, :]

    def forward_tail(b, c, conv):
        at = pl.ds(c * crow, crow)
        pair = jnp.concatenate(split(conv), axis=1)
        chl[b, at] = pair
        act, slope = silu_pair(expand(pair, in_dup[b], in_low[b]))
        dact[b, at] = slope
        ah[b, at], al[b, at] = split(act)

    def backward_head(b, c, g):
        at = pl.ds(c * crow, crow)
        pair = jnp.concatenate(split(g), axis=1)
        ghl[b, at] = pair
        high, low = split(expand(pair, outt_dup[b], outt_low[b]) * dact[b, at])
        ph[b, at], plo[b, at] = high, low
        return contract(high, low, int_cat[b])

    def weight_grads(b):
        both = dot(chl[b], ph[b], TN)
        gwi = both[0:128] + (both[128:256] + dot(chl[b, :, 0:128], plo[b], TN))
        gbuf[b, 0:128, :] = gwi[:, 0:128]
        gbuf[b, 128:256, :] = gwi[:, 128:256]
        both = dot(ghl[b], ah[b], TN)
        gwo = both[0:128] + (both[128:256] + dot(ghl[b, :, 0:128], al[b], TN))
        gbuf[b, 256:512, :] = gwo.T

    halo2 = [seg_halo(pad2, c) for c in range(CHUNKS)]
    waited = False
    for c in ORDER:
        if c in (0, CHUNKS - 1) and not waited:
            halo1.wait()
            waited = True
        conv = tap(0, 0) * gather(pad1, c, 0)
        for k in range(1, TAPS):
            conv = conv + tap(0, k) * gather(pad1, c, k * D1)
        forward_tail(0, c, conv)
        at = pl.ds(c * crow, crow)
        s = gather(x_ref.at[0], c, 0) + contract(ah[0, at], al[0, at], out_cat[0])
        st1[at] = s
        pad2[c, HALF:HALF + segs] = (s * inv_rms(s) * gain2).reshape(segs, RES, 128)
        halo2[c].start()

    loads[5].wait()

    ghalo2 = [seg_halo(gpad2, c) for c in range(CHUNKS)]
    for c in ORDER:
        halo2[c].wait()
        conv = tap(1, 0) * pad2[c, 0:segs].reshape(crow, 128)
        for k in range(1, TAPS):
            conv = conv + tap(1, k) * pad2[c, k:k + segs].reshape(crow, 128)
        forward_tail(1, c, conv)
        gconv = backward_head(1, c, gather(ct_ref.at[0], c, 0))
        gpad2[c, HALF:HALF + segs] = gconv.reshape(segs, RES, 128)
        ghalo2[c].start()

    half = grad_rows // nrep
    quarter = half // ndp
    piece = quarter // nctx
    axes = (
        (on_rep, ri, nrep, rec_a, sm_a, half, 0),
        (on_dp, di, ndp, rec_b, sm_b, quarter, ri * half),
        (on_ctx, zi, nctx, rec_c, sm_c, piece, ri * half + di * quarter),
    )

    def rows_at(start, size):
        return pl.ds(pl.multiple_of(start, 8), size)

    def scatter_start(b, level):
        place, me, n, rec, _, size, base = axes[level]
        copies = []
        for o in range(1, n):
            peer = lax.rem(me + o, n)
            copy = remote(
                gbuf.at[b, rows_at(base + peer * size, size)], rec.at[b, o - 1], place(peer)
            )
            copy.start()
            copies.append(copy)
        pending.append(copies)
        return copies

    def scatter_end(b, level, copies):
        place, me, n, rec, _, size, base = axes[level]
        own = rows_at(base + me * size, size)
        total = gbuf[b, own, :]
        for o in range(1, n):
            copies[o - 1].wait_recv()
            total = total + rec[b, o - 1]
        if level == 2:
            obuf[b, own, :] = total
        else:
            gbuf[b, own, :] = total

    def gather_start(b, level):
        place, me, n, _, _, size, base = axes[level]
        own = rows_at(base + me * size, size)
        copies = []
        for o in range(1, n):
            peer = lax.rem(me + o, n)
            copy = remote(obuf.at[b, own], obuf.at[b, own], place(peer))
            copy.start()
            copies.append(copy)
        pending.append(copies)
        return copies

    def arrive(copies):
        for copy in copies:
            copy.wait_recv()

    def small_start(level):
        place, me, n, _, slots, _, _ = axes[level]
        slots[me] = small[...]
        copies = []
        for o in range(1, n):
            peer = lax.rem(me + o, n)
            copy = remote(slots.at[me], slots.at[me], place(peer))
            copy.start()
            copies.append(copy)
        pending.append(copies)
        return copies

    def small_end(level, copies):
        n, slots = axes[level][2], axes[level][4]
        arrive(copies)
        total = slots[0]
        for i in range(1, n):
            total = total + slots[i]
        small[...] = total

    weight_grads(1)
    red2 = scatter_start(1, 0)
    for k in range(TAPS):
        total = jnp.zeros((1, 128), F32)
        for c in range(CHUNKS):
            both = gpad2[c, HALF:HALF + segs] * pad2[c, k:k + segs]
            total = total + jnp.sum(both.reshape(crow, 128), axis=0, keepdims=True)
        small[k:k + 1, :] = total

    gain_sum = jnp.zeros((1, 128), F32)
    for step, c in enumerate(ORDER):
        ghalo2[c].wait()
        at = pl.ds(c * crow, crow)
        gnorm = tap(1, TAPS - 1) * gpad2[c, 0:segs].reshape(crow, 128)
        for k in range(1, TAPS):
            gnorm = gnorm + tap(1, TAPS - 1 - k) * gpad2[c, k:k + segs].reshape(crow, 128)
        s = st1[at]
        r = inv_rms(s)
        xhat = s * r
        gain_sum = gain_sum + jnp.sum(gnorm * xhat, axis=0, keepdims=True)
        q = gnorm * gain2
        g = gather(ct_ref.at[0], c, 0) + r * (q - xhat * jnp.mean(q * xhat, axis=-1, keepdims=True))
        gconv = backward_head(0, c, g)
        for j in range(segs):
            lo = j * D2 + c * RES
            g1[lo:lo + RES, :] = g[j * RES:(j + 1) * RES, :]
            gpad1[rim + lo:rim + lo + RES, :] = gconv[j * RES:(j + 1) * RES, :]
        if step == 1:
            scatter_end(1, 0, red2)
            red2 = scatter_start(1, 1)
    small[7:8, :] = gain_sum
    ghalo1 = rim_halo(gpad1)
    ghalo1.start()
    weight_grads(0)
    red1 = scatter_start(0, 0)
    scatter_end(1, 1, red2)
    red2 = scatter_start(1, 2)
    for k in range(TAPS):
        both = gpad1[rim:rim + rows_total, :] * pad1[k * D1:k * D1 + rows_total, :]
        small[8 + k:9 + k, :] = jnp.sum(both, axis=0, keepdims=True)

    scatter_end(0, 0, red1)
    red1 = scatter_start(0, 1)

    gain_sum = jnp.zeros((1, 128), F32)
    waited = False
    blocks = rows_total // D2
    for q_i in [i for i in range(1, blocks - 1)] + [0, blocks - 1]:
        if q_i in (0, blocks - 1) and not waited:
            ghalo1.wait()
            waited = True
        lo = q_i * D2
        gnorm = tap(0, TAPS - 1) * gpad1[lo:lo + D2, :]
        for k in range(1, TAPS):
            gnorm = gnorm + tap(0, TAPS - 1 - k) * gpad1[lo + k * D1:lo + k * D1 + D2, :]
        s = x_ref[0, lo:lo + D2, :]
        r = inv_rms(s)
        xhat = s * r
        gain_sum = gain_sum + jnp.sum(gnorm * xhat, axis=0, keepdims=True)
        q = gnorm * gain1
        gx_ref[0, lo:lo + D2, :] = g1[lo:lo + D2, :] + r * (
            q - xhat * jnp.mean(q * xhat, axis=-1, keepdims=True)
        )
    small[15:16, :] = gain_sum

    def write_out(b):
        gwi_ref[b, :, 0:128] = obuf[b, 0:128, :]
        gwi_ref[b, :, 128:256] = obuf[b, 128:256, :]
        gwo_ref[b] = obuf[b, 256:512, :]

    tiny = small_start(0)
    scatter_end(1, 2, red2)
    all2 = gather_start(1, 2)
    scatter_end(0, 1, red1)
    red1 = scatter_start(0, 2)
    small_end(0, tiny)
    tiny = small_start(1)
    arrive(all2)
    all2 = gather_start(1, 1)
    scatter_end(0, 2, red1)
    all1 = gather_start(0, 2)
    small_end(1, tiny)
    tiny = small_start(2)
    arrive(all2)
    all2 = gather_start(1, 0)
    arrive(all1)
    all1 = gather_start(0, 1)
    small_end(2, tiny)
    arrive(all2)
    write_out(1)
    arrive(all1)
    all1 = gather_start(0, 0)
    for k in range(TAPS):
        gt_ref[k, 0:1, :] = small[8 + k:9 + k, :]
        gt_ref[k, 1:2, :] = small[k:k + 1, :]
    gg_ref[1:2, :] = small[7:8, :]
    gg_ref[0:1, :] = small[15:16, :]
    arrive(all1)
    write_out(0)

    for item in pending:
        if isinstance(item, list):
            for copy in item:
                copy.wait_send()
        else:
            item.finish()


def publish(*refs):
    srcs, dsts, sem = refs[:5], refs[5:10], refs[10]
    copies = [pltpu.make_async_copy(srcs[i], dsts[i], sem.at[i]) for i in range(5)]
    for copy in copies:
        copy.start()
    for copy in copies:
        copy.wait()


def local(nctx, ndp, nrep, features, cotangent, norm_gains, depth_taps, w_in, w_out):
    rows = features.shape[1]
    unit = 8 * nctx * ndp * nrep
    grad_rows = -(-512 // unit) * unit
    half = grad_rows // nrep
    quarter = half // ndp
    piece = quarter // nctx
    rim = HALF * D1
    wide = rows // D2 + 2 * HALF
    sems = 4 + 4 * CHUNKS + 5 * (nctx + ndp + nrep)
    vmem = pltpu.VMEM

    def peers(n):
        return max(n - 1, 1)

    taps = jnp.transpose(depth_taps, (1, 0, 2))
    args = tuple(
        pltpu.with_memory_space_constraint(a, pltpu.HBM)
        for a in (features, cotangent, norm_gains, taps, w_in, w_out)
    )
    shapes = tuple(
        jax.ShapeDtypeStruct(a.shape, F32) for a in (features, norm_gains, taps, w_in, w_out)
    )
    results = pl.pallas_call(
        functools.partial(kernel, nctx, ndp, nrep, rows, grad_rows),
        out_shape=shapes,
        in_specs=[pl.BlockSpec(memory_space=pltpu.HBM)] * 6,
        out_specs=tuple([pl.BlockSpec(memory_space=vmem)] * 5),
        scratch_shapes=[vmem(a.shape, F32) for a in args] + [
            pltpu.SemaphoreType.DMA((6,)),
            vmem((rows + 2 * rim, 128), F32),
            vmem((rows + 2 * rim, 128), F32),
            vmem((CHUNKS, wide, RES, 128), F32),
            vmem((CHUNKS, wide, RES, 128), F32),
            vmem((rows, 128), F32),
            vmem((rows, 128), F32),
            vmem((2, 256, 256), BF16),
            vmem((2, 128, 256), BF16),
            vmem((2, 256, 256), BF16),
            vmem((2, 256, 256), BF16),
            vmem((2, 128, 256), BF16),
            vmem((2, 256, 256), BF16),
            vmem((2, rows, 256), BF16),
            vmem((2, rows, 256), BF16),
            vmem((2, rows, 256), BF16),
            vmem((2, rows, 256), F32),
            vmem((2, rows, 256), BF16),
            vmem((2, rows, 256), BF16),
            vmem((2, rows, 256), BF16),
            vmem((2, grad_rows, 128), F32),
            vmem((2, grad_rows, 128), F32),
            vmem((2, peers(nrep), half, 128), F32),
            vmem((2, peers(ndp), quarter, 128), F32),
            vmem((2, peers(nctx), piece, 128), F32),
            vmem((16, 128), F32),
            vmem((nrep, 16, 128), F32),
            vmem((ndp, 16, 128), F32),
            vmem((nctx, 16, 128), F32),
            pltpu.SemaphoreType.DMA((sems,)),
            pltpu.SemaphoreType.DMA((sems,)),
        ],
        compiler_params=pltpu.CompilerParams(
            collective_id=0, has_side_effects=True, vmem_limit_bytes=40 * 1024 * 1024
        ),
    )(*args)
    gx, gg, gt, gwi, gwo = pl.pallas_call(
        publish,
        out_shape=shapes,
        in_specs=[pl.BlockSpec(memory_space=pl.ANY)] * 5,
        out_specs=tuple([pl.BlockSpec(memory_space=pltpu.HBM)] * 5),
        compiler_params=pltpu.CompilerParams(vmem_limit_bytes=4 * 1024 * 1024),
        scratch_shapes=[pltpu.SemaphoreType.DMA((5,))],
    )(*results)
    return gx, gg, jnp.transpose(gt, (1, 0, 2)), gwi, gwo


def solution(mesh):
    sizes = dict(mesh.shape)
    return jax.shard_map(
        functools.partial(local, sizes["ctx"], sizes["dp"], sizes["rep"]),
        mesh=mesh,
        in_specs=(
            P(("groups", "dp", "rep"), "ctx", None),
            P(("groups", "dp", "rep"), "ctx", None),
            P(),
            P(),
            P(),
            P(),
        ),
        out_specs=(
            P(("groups", "dp", "rep"), "ctx", None),
            P("groups", None),
            P("groups", None, None),
            P("groups", None, None),
            P("groups", None, None),
        ),
        check_vma=False,
    )
```
